32 devices in a mesh: expert: 8 (over y, x, core), dp: 4 (over z).
Axes of the slice: x: 2, y: 2, z: 4, core: 2. Of those that a mesh axis runs over, the one named last changes fastest.
Arguments:
- tokens: bfloat16 [4096, 2048], P(('expert', 'dp')), may hold values from -6 to 6
- cotangent: bfloat16 [4096, 2048], P(('expert', 'dp')), may hold values from -6 to 6
- router_probs: float32 [4096, 6], P(('expert', 'dp')), may hold values from 0.1 to 0.6
- routes: int32 [4096, 6], P(('expert', 'dp')), may hold values from 0 to 15, all different within a row; in each aligned block of 128 rows (0 to 127, 128 to 255, ...) at most 60 rows name the same one
- partner: int32 [8], replicated, may hold values from 0 to 7, as said below
- gate_weight: bfloat16 [16, 2048, 768], P('expert'), may hold values from -0.125 to 0.125
- up_weight: bfloat16 [16, 2048, 768], P('expert'), may hold values from -0.125 to 0.125
- down_weight: bfloat16 [16, 768, 2048], P('expert'), may hold values from -0.21875 to 0.21875
Outputs:
- output: bfloat16 [4096, 2048], P(('expert', 'dp'))
- token_grad: bfloat16 [4096, 2048], P(('expert', 'dp'))
- expert_grads: bfloat16 [768, 16, 3, 2048], P('dp', 'expert')
The draws below stay inside these ranges and needn't reach their ends.
Inputs may be any that keep to these rules, and one draw needn't show every extreme that they name: `routes`: each token names 6 different experts. Within the 128 rows of one device no expert is named by more than 60 rows, a bound that some block reaches of them. partner[j] is j or (j + 4) mod 8, and partner[partner[j]] = j.
All inputs are finite; a program needn't handle non-finite values.
Results may differ from the reference program's by a relative error of at most 0.0095.
Values may be sent and summed in bfloat16 or wider, within the bound.
A program may use at most 192 MiB of HBM per device.

```python
import math
import jax
import jax.numpy as jnp
import numpy as np
from jax import lax

D = 2048
FF = 768
TOK_DEV = 128
TOPK = 6
EXP_DEV = 2
EXPERTS = 16
CAP = 60
TOKENS = 4096
N_EXPERT = 8
N_DP = 4


def draw_partner(key, part):
    half_axis = N_EXPERT // 2
    flags = jax.random.randint(key, (half_axis,), 0, 2)
    flags = jnp.concatenate([flags, flags])
    position = jnp.arange(N_EXPERT)
    return jnp.where(flags == 1, (position + half_axis) % N_EXPERT, position).astype(jnp.int32)


def level_of(own_key, dims, pieces, least, high):
    def one(axis_at, shards_of):
        heights = jax.random.uniform(jax.random.fold_in(jax.random.fold_in(own_key, 6), axis_at), (shards_of,), jnp.float32, least / len(pieces), high / len(pieces))
        return jnp.repeat(jnp.exp(heights), dims[axis_at] // shards_of).reshape((-1,) + (1,) * (len(dims) - axis_at - 1))

    loudness = one(*pieces[0])
    for cut in pieces[1:]:
        loudness = loudness * one(*cut)
    return loudness


def shared_out(stream_key, own, number, rows, count, top, limit, skew):
    sequence = jax.random.permutation(stream_key, count)
    crowded, usual = load_shares(count, rows * top, limit, skew, True), load_shares(count, rows * top, limit, skew, False)
    places = jnp.arange(count)

    def named(lengths, offset_by):
        used = int((lengths > 0).sum())
        fixed = max(1, used // 4)
        moved = fixed + (places - fixed + offset_by * (used - fixed)) % max(1, count - fixed)
        return jnp.zeros((count,), jnp.int32).at[sequence[jnp.where(places < fixed, places, moved)]].set(jnp.asarray(lengths, jnp.int32))

    lengths = jnp.where(number % 4 == 0, named(crowded, number // 4), named(usual, number - number // 4 - 1))
    mixed = jax.random.permutation(jax.random.fold_in(own, 3), count)
    donor, sink = mixed[0:count // 2 * 2:2], mixed[1:count // 2 * 2:2]
    slack = jnp.minimum(lengths[donor] - 1, limit - lengths[sink]) // 2
    slack = jnp.where((donor == sequence[0]) | (sink == sequence[0]) | (lengths[sink] == 0), 0, jnp.maximum(slack, 0))
    moved = jax.random.randint(jax.random.fold_in(own, 4), (count // 2,), 0, 1 << 20) % (slack + 1)
    lengths = lengths.at[donor].add(-moved).at[sink].add(moved)
    items = jnp.searchsorted(jnp.cumsum(lengths), jnp.arange(rows * top), side="right").astype(jnp.int32)
    grid = items.reshape(top, rows).T
    grid = grid[jax.random.permutation(jax.random.fold_in(own, 1), rows)]
    offset_by = jax.random.randint(jax.random.fold_in(own, 2), (rows, 1), 0, top)
    return jnp.take_along_axis(grid, (jnp.arange(top)[None, :] + offset_by) % top, axis=1)


def load_shares(number_of, total, bound, skew, full):
    weights = [(1 << 20) // math.isqrt(standing ** skew) + 1 for standing in range(1, number_of + 1)]
    largest = bound if full else min(bound, max(-(-total // number_of), total * weights[0] // sum(weights)))
    least = 1 if total - largest >= number_of - 1 else 0
    given, spare = [largest] + [least] * (number_of - 1), total - largest - least * (number_of - 1)
    while spare > 0:
        free = [i for i in range(1, number_of) if given[i] < largest] or [i for i in range(1, number_of) if given[i] < bound]
        mass, left = sum([weights[i] for i in free]), spare
        for i in free:
            more = min(bound - given[i], max(1, left * weights[i] // mass), spare)
            given[i] = given[i] + more
            spare = spare - more
    return np.array(given)


def gaussian(key, dims, deviation, reach, cuts=(), kind=jnp.bfloat16):
    drawn = jax.random.normal(key, dims, jnp.float32) * deviation
    if len(cuts) > 0:
        drawn = level_of(key, dims, cuts, -0.22, 0.18) * drawn
    return jnp.clip(drawn, min=-reach, max=reach).astype(kind)


def setup_inputs(seed: int = 0) -> dict:
    key_of = jax.random.split(jax.random.key(seed), 9)
    tokens = gaussian(key_of[0], (TOKENS, D), 1.0, 6.0, ((0, 32),))
    cotangent = gaussian(key_of[1], (TOKENS, D), 1.0, 6.0, ((0, 32),))
    router_probs = jnp.clip(0.1 + 0.5 * jax.random.uniform(key_of[2], (TOKENS, TOPK), jnp.float32) ** level_of(key_of[2], (TOKENS, TOPK), ((0, 32),), -0.2, 0.2), 0.1, 0.6)
    routes_keys = jax.random.split(jax.random.fold_in(key_of[3], 1), TOKENS // TOK_DEV)
    routes_turns = jax.random.permutation(jax.random.fold_in(key_of[3], 3), TOKENS // TOK_DEV)
    routes = jax.vmap(lambda own, number: shared_out(jax.random.fold_in(key_of[3], 2), own, number, TOK_DEV, EXPERTS, TOPK, CAP, 2))(routes_keys, routes_turns).reshape((TOKENS, TOPK))
    partner = draw_partner(jax.random.fold_in(key_of[8], 71), 0)
    gate_weight = gaussian(key_of[5], (EXPERTS, D, FF), D ** -0.5, 0.125, ((0, 8),))
    up_weight = gaussian(key_of[6], (EXPERTS, D, FF), D ** -0.5, 0.125, ((0, 8),))
    down_weight = gaussian(key_of[7], (EXPERTS, FF, D), FF ** -0.5, 0.21875, ((0, 8),))
    return dict(tokens=tokens, cotangent=cotangent, router_probs=router_probs, routes=routes, partner=partner, gate_weight=gate_weight, up_weight=up_weight, down_weight=down_weight)


def reference(tokens, cotangent, router_probs, routes, partner, gate_weight, up_weight, down_weight):
    assigned = TOKENS * TOPK
    flat_routes = routes.reshape(-1).astype(jnp.int32)
    token_of = (jnp.arange(assigned, dtype=jnp.int32) // TOPK).astype(jnp.int32)
    group_of = ((token_of // TOK_DEV) % N_DP).astype(jnp.int32)
    sort_key = (flat_routes * N_DP + group_of).astype(jnp.int32)
    sorted_at = jnp.argsort(sort_key, stable=True).astype(jnp.int32)
    bin_count = EXPERTS * N_DP
    counts = jnp.sum((sort_key[None, :] == jnp.arange(bin_count, dtype=jnp.int32)[:, None]).astype(jnp.int32), axis=1)
    starts = (jnp.cumsum(counts) - counts).astype(jnp.int32)
    most_rows = CAP * N_EXPERT
    padded_order = jnp.concatenate([sorted_at, jnp.full((most_rows,), assigned, jnp.int32)])
    zero_row = jnp.zeros((1, D), tokens.dtype)
    padded_tokens = jnp.concatenate([tokens, zero_row], axis=0)
    padded_cot = jnp.concatenate([cotangent, zero_row], axis=0)
    padded_probs = jnp.concatenate([router_probs.reshape(-1), jnp.zeros((1,), jnp.float32)])
    position = jnp.arange(most_rows, dtype=jnp.int32)

    def per_expert(expert):
        slot_id = (partner[expert // EXP_DEV] * EXP_DEV + expert % EXP_DEV).astype(jnp.int32)
        gate_w = gate_weight[slot_id].astype(jnp.float32)
        up_w = up_weight[slot_id].astype(jnp.float32)
        down_w = down_weight[slot_id].astype(jnp.float32)
        out_list = []
        dx_list = []
        index_list = []
        grad_total = jnp.zeros((3, FF, D), jnp.float32)
        for group_id in range(N_DP):
            begin_at = starts[expert * N_DP + group_id]
            live_count = counts[expert * N_DP + group_id]
            row_index = lax.dynamic_slice(padded_order, (begin_at,), (most_rows,))
            row_index = jnp.where(position < live_count, row_index, assigned).astype(jnp.int32)
            row_token = (row_index // TOPK).astype(jnp.int32)
            expert_in = padded_tokens[row_token].astype(jnp.float32)
            scaled = (padded_probs[row_index][:, None] * padded_cot[row_token].astype(jnp.float32)).astype(jnp.bfloat16)
            expert_cot = lax.optimization_barrier(scaled).astype(jnp.float32)
            gate_pre = jnp.dot(expert_in, gate_w, preferred_element_type=jnp.float32)
            up_proj = jnp.dot(expert_in, up_w, preferred_element_type=jnp.float32)
            sigmoid_gate = jax.nn.sigmoid(gate_pre)
            activated = gate_pre * sigmoid_gate
            hidden = lax.optimization_barrier((activated * up_proj).astype(jnp.bfloat16)).astype(jnp.float32)
            out_rows = jnp.dot(hidden, down_w, preferred_element_type=jnp.float32).astype(jnp.bfloat16)
            grad_hidden = jnp.dot(expert_cot, down_w.T, preferred_element_type=jnp.float32)
            grad_gate = (grad_hidden * up_proj * sigmoid_gate * (1.0 + gate_pre * (1.0 - sigmoid_gate))).astype(jnp.bfloat16)
            grad_up = (grad_hidden * activated).astype(jnp.bfloat16)
            grad_gate = lax.optimization_barrier(grad_gate).astype(jnp.float32)
            grad_up = lax.optimization_barrier(grad_up).astype(jnp.float32)
            dx_rows = (jnp.dot(grad_gate, gate_w.T, preferred_element_type=jnp.float32)
                       + jnp.dot(grad_up, up_w.T, preferred_element_type=jnp.float32)).astype(jnp.bfloat16)
            partial_value = jnp.stack([
                jnp.dot(grad_gate.T, expert_in, preferred_element_type=jnp.float32),
                jnp.dot(grad_up.T, expert_in, preferred_element_type=jnp.float32),
                jnp.dot(hidden.T, expert_cot, preferred_element_type=jnp.float32)], axis=0)
            partial_value = lax.optimization_barrier(partial_value.astype(jnp.bfloat16))
            grad_total = grad_total + partial_value.astype(jnp.float32)
            out_list.append(out_rows)
            dx_list.append(dx_rows)
            index_list.append(row_index)
        return (jnp.stack(out_list), jnp.stack(dx_list), jnp.stack(index_list), grad_total.astype(jnp.bfloat16))

    out_rows, dx_rows, indices, grads = lax.map(per_expert, jnp.arange(EXPERTS, dtype=jnp.int32))
    flat_index = indices.reshape(-1)
    assign_out = jnp.zeros((assigned + 1, D), jnp.bfloat16).at[flat_index].set(out_rows.reshape(-1, D).astype(jnp.bfloat16))
    assign_dx = jnp.zeros((assigned + 1, D), jnp.bfloat16).at[flat_index].set(dx_rows.reshape(-1, D).astype(jnp.bfloat16))
    picked_out = assign_out[:assigned].reshape(TOKENS, TOPK, D).astype(jnp.float32)
    picked_dx = assign_dx[:assigned].reshape(TOKENS, TOPK, D).astype(jnp.float32)
    output = jnp.sum(router_probs[:, :, None] * picked_out, axis=1).astype(jnp.bfloat16)
    token_grad = jnp.sum(picked_dx, axis=1).astype(jnp.bfloat16)
    expert_grads = jnp.transpose(grads, (2, 0, 1, 3))
    return (output, token_grad, expert_grads)
```

```python
import jax
import jax.numpy as jnp
from jax import lax
from jax.sharding import PartitionSpec as P

BF = jnp.bfloat16
F32 = jnp.float32


def dot(a, b, dims):
    return lax.dot_general(a, b, (dims, ((), ())), preferred_element_type=F32)


def pick(onehot, block):
    rows = lax.dot_general(onehot, block, (((2,), (1,)), ((0,), (0,))), preferred_element_type=F32)
    return rows.reshape(-1, rows.shape[-1])


def select(routes, probs, expert, capacity):
    tok = routes.shape[2]
    hit = routes == expert
    mask = jnp.any(hit, axis=1)
    prob = jnp.sum(jnp.where(hit, probs, 0.0), axis=1)
    lower = (jnp.arange(tok)[:, None] <= jnp.arange(tok)[None, :]).astype(BF)
    rank = dot(mask.astype(BF), lower, ((1,), (0,))) - 1.0
    chosen = (rank[:, None, :] == jnp.arange(capacity, dtype=F32)[None, :, None]) & mask[:, None, :]
    row_prob = jnp.sum(jnp.where(chosen, prob[:, None, :], 0.0), axis=2)
    return chosen.astype(BF), row_prob.reshape(-1, 1)


def acts(x, c, gate_w, up_w, down_w):
    gate_pre = dot(x, gate_w, ((1,), (0,)))
    up_proj = dot(x, up_w, ((1,), (0,)))
    grad_hidden = dot(c, down_w, ((1,), (1,)))
    sig = jax.nn.sigmoid(gate_pre)
    active = gate_pre * sig
    hidden = (active * up_proj).astype(BF)
    dgate = (grad_hidden * up_proj * sig * (1.0 + gate_pre * (1.0 - sig))).astype(BF)
    dup = (grad_hidden * active).astype(BF)
    return dgate, dup, hidden


def local(tokens, cotangent, router_probs, routes, partner, gate_weight, up_weight, down_weight):
    tok, width = tokens.shape
    top = routes.shape[1]
    exp_dev = gate_weight.shape[0]
    units = gate_weight.shape[2]
    owners = lax.axis_size("expert")
    n_dp = lax.axis_size("dp")
    far = n_dp // 2
    capacity = max(2, 5 * tok * top // (4 * exp_dev * owners))
    capacity = -(-capacity // 16) * 16
    row_here = lax.axis_index("expert")
    z = lax.axis_index("dp")
    partner_here = jnp.sum(jnp.where(jnp.arange(owners) == row_here, partner, 0))
    half = units // far
    part_at = (z // 2) * half

    aux = jnp.concatenate([router_probs, routes.astype(F32)], axis=1).T
    aux_all = lax.all_gather(aux, ("expert", "dp"), axis=0).reshape(owners, n_dp, 2 * top, tok)

    def gathered(shift):
        moved = (tokens, cotangent)
        if shift:
            pairs = [((i + shift) % n_dp, i) for i in range(n_dp)]
            moved = tuple(lax.ppermute(v, "dp", pairs) for v in moved)
        x_all, c_all = (lax.all_gather(v, "expert", axis=0) for v in moved)
        own = lax.dynamic_index_in_dim(aux_all, lax.rem(z + shift, n_dp), 1, keepdims=False)
        return x_all, c_all, own[:, :top], own[:, top:]

    sets = [gathered(2 * h) for h in range(far)]

    outs, dxs, chosens = [], [], []
    pieces = []
    for s in range(exp_dev):
        expert = (partner_here * exp_dev + s).astype(F32)
        gate_w, up_w, down_w = gate_weight[s], up_weight[s], down_weight[s]
        lists = ([], [], [])
        rows = []
        for h, (x_all, c_all, probs, names) in enumerate(sets):
            chosen, row_prob = select(names, probs, expert, capacity)
            x = pick(chosen, x_all).astype(BF)
            c = (pick(chosen, c_all) * row_prob).astype(BF)
            if h == 0:
                dgate, dup, hidden = acts(x, c, gate_w, up_w, down_w)
                out = (dot(hidden, down_w, ((1,), (0,))) * row_prob).astype(BF)
                dx = (dot(dgate, gate_w, ((1,), (1,))) + dot(dup, up_w, ((1,), (1,)))).astype(BF)
                outs.append(out.reshape(owners, capacity, width))
                dxs.append(dx.reshape(owners, capacity, width))
                chosens.append(chosen)
                dgate, dup, hidden = (
                    lax.dynamic_slice_in_dim(v, part_at, half, 1) for v in (dgate, dup, hidden)
                )
            else:
                dgate, dup, hidden = acts(
                    x,
                    c,
                    lax.dynamic_slice_in_dim(gate_w, part_at, half, 1),
                    lax.dynamic_slice_in_dim(up_w, part_at, half, 1),
                    lax.dynamic_slice_in_dim(down_w, part_at, half, 0),
                )
            for kept, v in zip(lists, (dgate, dup, hidden)):
                kept.append(v)
            rows.append((x, x, c))
        for m in range(3):
            total = None
            for h in range(far):
                term = dot(lists[m][h], rows[h][m], ((0,), (0,)))
                total = term if total is None else total + term
            pieces.append(total.astype(BF))

    chosen = jnp.concatenate(chosens, axis=1)

    def back(values):
        stacked = jnp.concatenate(values, axis=1)
        summed = lax.dot_general(
            chosen, stacked, (((1,), (1,)), ((0,), (0,))), preferred_element_type=F32
        ).astype(BF)
        return lax.psum_scatter(summed, "expert", scatter_dimension=0, tiled=False)

    output = back(outs)
    token_grad = back(dxs)

    quarter = half // 2
    mine = lax.rem(z, 2)
    near = [(i, i ^ 1) for i in range(n_dp)]
    across = [(i, i ^ (owners // 2)) for i in range(owners)]
    finished = []
    for piece in pieces:
        kept = lax.dynamic_slice_in_dim(piece, mine * quarter, quarter, 0)
        sent = lax.dynamic_slice_in_dim(piece, (1 - mine) * quarter, quarter, 0)
        came = lax.ppermute(sent, "dp", near)
        summed = (kept.astype(F32) + came.astype(F32)).astype(BF)
        swapped = lax.ppermute(summed, "expert", across)
        finished.append(jnp.where(partner_here == row_here, summed, swapped))
    grads = jnp.stack(finished, axis=1).reshape(quarter, exp_dev, 3, width)
    return (output, token_grad, grads)


def solution(mesh):
    rows = P(("expert", "dp"), None)
    return jax.shard_map(
        local,
        mesh=mesh,
        in_specs=(rows, rows, rows, rows, P(), *[P("expert", None, None)] * 3),
        out_specs=(rows, rows, P("dp", "expert", None, None)),
        check_vma=False,
    )
```

```python
import functools

import jax
import jax.numpy as jnp
from jax import lax
from jax.experimental import pallas as pl
from jax.experimental.pallas import tpu as pltpu
from jax.sharding import PartitionSpec as P

BF = jnp.bfloat16
F32 = jnp.float32


def flip(index, bit):
    return index + bit * (1 - 2 * ((index // bit) % 2))


def flip_all(index, mask):
    bit = 1
    while bit <= mask:
        if mask & bit:
            index = flip(index, bit)
        bit *= 2
    return index


def gather_kernel(owners, n_dp, *refs):
    ins, outs = refs[:3], refs[3:6]
    send_sem, recv_sem, local_sem = refs[6:]
    far = n_dp // 2
    me = lax.axis_index("expert")
    z = lax.axis_index("dp")
    bits = [1 << i for i in range(1, owners.bit_length() - 1)]

    barrier = pltpu.get_barrier_semaphore()
    for bit in [1] + bits:
        pl.semaphore_signal(
            barrier, device_id={"expert": flip(me, bit)}, device_id_type=pl.DeviceIdType.MESH
        )
    for h in range(1, far):
        pl.semaphore_signal(
            barrier, device_id={"dp": (z + 2 * h) % n_dp}, device_id_type=pl.DeviceIdType.MESH
        )
    pl.semaphore_wait(barrier, len(bits) + far)

    number = 0
    started = []
    arrival = {}

    def send(src, dst, target, key):
        nonlocal number
        copy = pltpu.make_async_remote_copy(
            src_ref=src,
            dst_ref=dst,
            send_sem=send_sem.at[number],
            recv_sem=recv_sem.at[number],
            device_id=target,
            device_id_type=pl.DeviceIdType.MESH,
        )
        copy.start()
        number += 1
        started.append(copy)
        arrival[key] = copy

    landed = set()

    def need(key):
        if key in arrival and key not in landed:
            arrival[key].wait_recv()
            landed.add(key)

    order = (2, 0, 1)
    own = []
    for a in order:
        for h in range(1, far):
            send(
                ins[a],
                outs[a].at[h, me],
                {"dp": (z - 2 * h + n_dp) % n_dp},
                (a, h, 0),
            )
        own.append(pltpu.make_async_copy(ins[a], outs[a].at[0, me], local_sem.at[a]))
    ways = (bits, bits[::-1], bits[::-1])
    for step in range(len(bits) + 1):
        for h in range(far):
            for a in order:
                way = list(ways[a]) + [1]
                bit = way[step]
                for pick_at in range(1 << step):
                    mask = sum(way[i] for i in range(step) if pick_at >> i & 1)
                    need((a, h, mask))
                    at = flip_all(me, mask)
                    src = ins[a] if h == 0 and mask == 0 else outs[a].at[h, at]
                    send(src, outs[a].at[h, at], {"expert": flip(me, bit)}, (a, h, mask + bit))
        if step == 0:
            for copy in own:
                copy.start()
    for key in arrival:
        need(key)
    for copy in started:
        copy.wait_send()
    for copy in own:
        copy.wait()


def gather(tokens, cotangent, aux, owners, n_dp):
    far = n_dp // 2
    copies = 3 * (far * (owners - 1) + far - 1)
    ins = (tokens, cotangent, aux)
    return pl.pallas_call(
        functools.partial(gather_kernel, owners, n_dp),
        out_shape=[jax.ShapeDtypeStruct((far, owners, *v.shape), v.dtype) for v in ins],
        in_specs=[pl.BlockSpec(memory_space=pltpu.VMEM)] * 3,
        out_specs=[pl.BlockSpec(memory_space=pl.ANY)] * 3,
        scratch_shapes=[
            pltpu.SemaphoreType.DMA((copies,)),
            pltpu.SemaphoreType.DMA((copies,)),
            pltpu.SemaphoreType.DMA((3,)),
        ],
        compiler_params=pltpu.CompilerParams(collective_id=0, has_side_effects=True),
    )(*ins)


def dot(a, b, dims):
    return lax.dot_general(a, b, (dims, ((), ())), preferred_element_type=F32)


def pick(onehot, block):
    rows = lax.dot_general(onehot, block, (((2,), (1,)), ((0,), (0,))), preferred_element_type=F32)
    return rows.reshape(-1, rows.shape[-1])


def select(routes, probs, expert, capacity):
    tok = routes.shape[2]
    hit = routes == expert
    mask = jnp.any(hit, axis=1)
    prob = jnp.sum(jnp.where(hit, probs, 0.0), axis=1)
    lower = (jnp.arange(tok)[:, None] <= jnp.arange(tok)[None, :]).astype(BF)
    rank = dot(mask.astype(BF), lower, ((1,), (0,))) - 1.0
    chosen = (rank[:, None, :] == jnp.arange(capacity, dtype=F32)[None, :, None]) & mask[:, None, :]
    row_prob = jnp.sum(jnp.where(chosen, prob[:, None, :], 0.0), axis=2)
    return chosen.astype(BF), row_prob.reshape(-1, 1)


def acts(x, c, gate_w, up_w, down_w):
    gate_pre = dot(x, gate_w, ((1,), (0,)))
    up_proj = dot(x, up_w, ((1,), (0,)))
    grad_hidden = dot(c, down_w, ((1,), (1,)))
    sig = jax.nn.sigmoid(gate_pre)
    active = gate_pre * sig
    hidden = (active * up_proj).astype(BF)
    dgate = (grad_hidden * up_proj * sig * (1.0 + gate_pre * (1.0 - sig))).astype(BF)
    dup = (grad_hidden * active).astype(BF)
    return dgate, dup, hidden


def local(tokens, cotangent, router_probs, routes, partner, gate_weight, up_weight, down_weight):
    tok, width = tokens.shape
    top = routes.shape[1]
    exp_dev = gate_weight.shape[0]
    units = gate_weight.shape[2]
    owners = lax.axis_size("expert")
    n_dp = lax.axis_size("dp")
    far = n_dp // 2
    capacity = max(2, 5 * tok * top // (4 * exp_dev * owners))
    capacity = -(-capacity // 16) * 16
    row_here = lax.axis_index("expert")
    z = lax.axis_index("dp")
    partner_here = jnp.sum(jnp.where(jnp.arange(owners) == row_here, partner, 0))
    half = units // far
    part_at = (z // 2) * half

    spare = -(2 * top) % 8
    aux = jnp.concatenate([router_probs.T, routes.T.astype(F32), jnp.zeros((spare, tok), F32)])
    x_all, c_all, aux_all = gather(tokens, cotangent, aux, owners, n_dp)

    picks, later, pieces = [], [], []
    for s in range(exp_dev):
        expert = (partner_here * exp_dev + s).astype(F32)
        gate_w, up_w, down_w = gate_weight[s], up_weight[s], down_weight[s]
        lists = ([], [], [])
        rows = []
        for h in range(far):
            probs, names = aux_all[h, :, :top], aux_all[h, :, top : 2 * top]
            chosen, row_prob = select(names, probs, expert, capacity)
            if h == 0:
                picks.append(chosen)
            if pieces:
                chosen, _ = lax.optimization_barrier((chosen, pieces[-1]))
            x = pick(chosen, x_all[h]).astype(BF)
            c = (pick(chosen, c_all[h]) * row_prob).astype(BF)
            if h == 0:
                dgate, dup, hidden = acts(x, c, gate_w, up_w, down_w)
                later.append((dgate, dup, hidden, row_prob))
                dgate, dup, hidden = (
                    lax.dynamic_slice_in_dim(v, part_at, half, 1) for v in (dgate, dup, hidden)
                )
            else:
                dgate, dup, hidden = acts(
                    x,
                    c,
                    lax.dynamic_slice_in_dim(gate_w, part_at, half, 1),
                    lax.dynamic_slice_in_dim(up_w, part_at, half, 1),
                    lax.dynamic_slice_in_dim(down_w, part_at, half, 0),
                )
            for kept, v in zip(lists, (dgate, dup, hidden)):
                kept.append(v)
            rows.append((x, x, c))
        for m in range(3):
            total = None
            for h in range(far):
                term = dot(lists[m][h], rows[h][m], ((0,), (0,)))
                total = term if total is None else total + term
            pieces.append(total.astype(BF))

    chosen = jnp.concatenate(picks, axis=1)
    outs, dxs = [], []
    for s in range(exp_dev):
        dgate, dup, hidden, row_prob = later[s]
        dgate, dup, hidden, _ = lax.optimization_barrier((dgate, dup, hidden, pieces[-1]))
        out = (dot(hidden, down_weight[s], ((1,), (0,))) * row_prob).astype(BF)
        dx = dot(dgate, gate_weight[s], ((1,), (1,))) + dot(dup, up_weight[s], ((1,), (1,)))
        outs.append(out.reshape(owners, capacity, width))
        dxs.append(dx.astype(BF).reshape(owners, capacity, width))

    def back(values):
        stacked = jnp.concatenate(values, axis=1)
        summed = lax.dot_general(
            chosen, stacked, (((1,), (1,)), ((0,), (0,))), preferred_element_type=F32
        ).astype(BF)
        return lax.psum_scatter(summed, "expert", scatter_dimension=0, tiled=False)

    output = back(outs)
    token_grad = back(dxs)

    quarter = half // 2
    mine = lax.rem(z, 2)
    near = [(i, i ^ 1) for i in range(n_dp)]
    across = [(i, i ^ (owners // 2)) for i in range(owners)]
    finished = []
    for piece in pieces:
        kept = lax.dynamic_slice_in_dim(piece, mine * quarter, quarter, 0)
        sent = lax.dynamic_slice_in_dim(piece, (1 - mine) * quarter, quarter, 0)
        came = lax.ppermute(sent, "dp", near)
        summed = (kept.astype(F32) + came.astype(F32)).astype(BF)
        swapped = lax.ppermute(summed, "expert", across)
        finished.append(jnp.where(partner_here == row_here, summed, swapped))
    grads = jnp.stack(finished, axis=1).reshape(quarter, exp_dev, 3, width)
    return (output, token_grad, grads)


def solution(mesh):
    rows = P(("expert", "dp"), None)
    return jax.shard_map(
        local,
        mesh=mesh,
        in_specs=(rows, rows, rows, rows, P(), *[P("expert", None, None)] * 3),
        out_specs=(rows, rows, P("dp", "expert", None, None)),
        check_vma=False,
    )
```

```python
import functools

import jax
import jax.numpy as jnp
from jax import lax
from jax.experimental import pallas as pl
from jax.experimental.pallas import tpu as pltpu
from jax.sharding import PartitionSpec as P

BF = jnp.bfloat16
F32 = jnp.float32


def flip(index, bit):
    return index + bit * (1 - 2 * ((index // bit) % 2))


def flip_all(index, mask):
    bit = 1
    while bit <= mask:
        if mask & bit:
            index = flip(index, bit)
        bit *= 2
    return index


def gather_kernel(owners, n_dp, *refs):
    ins, outs = refs[:3], refs[3:6]
    send_sem, recv_sem, local_sem = refs[6:]
    far = n_dp // 2
    me = lax.axis_index("expert")
    z = lax.axis_index("dp")
    bits = [1 << i for i in range(1, owners.bit_length() - 1)]

    barrier = pltpu.get_barrier_semaphore()
    for bit in [1] + bits:
        pl.semaphore_signal(
            barrier, device_id={"expert": flip(me, bit)}, device_id_type=pl.DeviceIdType.MESH
        )
    for h in range(1, far):
        pl.semaphore_signal(
            barrier, device_id={"dp": (z + 2 * h) % n_dp}, device_id_type=pl.DeviceIdType.MESH
        )
    pl.semaphore_wait(barrier, len(bits) + far)

    number = 0
    started = []
    arrival = {}

    def send(src, dst, target, key):
        nonlocal number
        copy = pltpu.make_async_remote_copy(
            src_ref=src,
            dst_ref=dst,
            send_sem=send_sem.at[number],
            recv_sem=recv_sem.at[number],
            device_id=target,
            device_id_type=pl.DeviceIdType.MESH,
        )
        copy.start()
        number += 1
        started.append(copy)
        arrival[key] = copy

    landed = set()

    def need(key):
        if key in arrival and key not in landed:
            arrival[key].wait_recv()
            landed.add(key)

    order = (2, 0, 1)
    own = []
    for a in order:
        for h in range(1, far):
            send(
                ins[a],
                outs[a].at[h, me],
                {"dp": (z - 2 * h + n_dp) % n_dp},
                (a, h, 0),
            )
        own.append(pltpu.make_async_copy(ins[a], outs[a].at[0, me], local_sem.at[a]))
    ways = (bits, bits[::-1], bits[::-1])
    depth = len(bits)

    def forward(a, h, mask, bit):
        need((a, h, mask))
        at = flip_all(me, mask)
        src = ins[a] if h == 0 and mask == 0 else outs[a].at[h, at]
        send(src, outs[a].at[h, at], {"expert": flip(me, bit)}, (a, h, mask + bit))

    def masks(a, lo, hi):
        way = ways[a]
        return [sum(way[i] for i in range(depth) if p >> i & 1) for p in range(lo, hi)]

    def spread(h, a, step):
        for mask in masks(a, 0, 1 << step):
            forward(a, h, mask, ways[a][step])

    def sibling(h, a, step):
        for mask in masks(a, (1 << step) // 2, 1 << step):
            forward(a, h, mask, 1)

    for step in range(depth):
        for a in order:
            spread(0, a, step)
        for a in order:
            sibling(0, a, step)
    for copy in own:
        copy.start()
    for h in range(1, far):
        for a in order:
            spread(h, a, 0)
            sibling(h, a, 0)
    for a in order:
        sibling(0, a, depth)
    for h in range(1, far):
        for step in range(1, depth):
            for a in order:
                spread(h, a, step)
                sibling(h, a, step)
        for a in order:
            sibling(h, a, depth)
    for key in arrival:
        need(key)
    for copy in started:
        copy.wait_send()
    for copy in own:
        copy.wait()


def gather(tokens, cotangent, aux, owners, n_dp):
    far = n_dp // 2
    copies = 3 * (far * (owners - 1) + far - 1)
    ins = (tokens, cotangent, aux)
    return pl.pallas_call(
        functools.partial(gather_kernel, owners, n_dp),
        out_shape=[jax.ShapeDtypeStruct((far, owners, *v.shape), v.dtype) for v in ins],
        in_specs=[pl.BlockSpec(memory_space=pltpu.VMEM)] * 3,
        out_specs=[pl.BlockSpec(memory_space=pl.ANY)] * 3,
        scratch_shapes=[
            pltpu.SemaphoreType.DMA((copies,)),
            pltpu.SemaphoreType.DMA((copies,)),
            pltpu.SemaphoreType.DMA((3,)),
        ],
        compiler_params=pltpu.CompilerParams(collective_id=0, has_side_effects=True),
    )(*ins)


def dot(a, b, dims):
    return lax.dot_general(a, b, (dims, ((), ())), preferred_element_type=F32)


def pick(onehot, block):
    rows = lax.dot_general(onehot, block, (((2,), (1,)), ((0,), (0,))), preferred_element_type=F32)
    return rows.reshape(-1, rows.shape[-1])


def select(routes, probs, expert, capacity):
    tok = routes.shape[2]
    hit = routes == expert
    mask = jnp.any(hit, axis=1)
    prob = jnp.sum(jnp.where(hit, probs, 0.0), axis=1)
    lower = (jnp.arange(tok)[:, None] <= jnp.arange(tok)[None, :]).astype(BF)
    rank = dot(mask.astype(BF), lower, ((1,), (0,))) - 1.0
    chosen = (rank[:, None, :] == jnp.arange(capacity, dtype=F32)[None, :, None]) & mask[:, None, :]
    row_prob = jnp.sum(jnp.where(chosen, prob[:, None, :], 0.0), axis=2)
    return chosen.astype(BF), row_prob.reshape(-1, 1)


def acts(x, c, gate_w, up_w, down_w):
    gate_pre = dot(x, gate_w, ((1,), (0,)))
    up_proj = dot(x, up_w, ((1,), (0,)))
    grad_hidden = dot(c, down_w, ((1,), (1,)))
    sig = jax.nn.sigmoid(gate_pre)
    active = gate_pre * sig
    hidden = (active * up_proj).astype(BF)
    dgate = (grad_hidden * up_proj * sig * (1.0 + gate_pre * (1.0 - sig))).astype(BF)
    dup = (grad_hidden * active).astype(BF)
    return dgate, dup, hidden


def local(tokens, cotangent, router_probs, routes, partner, gate_weight, up_weight, down_weight):
    tok, width = tokens.shape
    top = routes.shape[1]
    exp_dev = gate_weight.shape[0]
    units = gate_weight.shape[2]
    owners = lax.axis_size("expert")
    n_dp = lax.axis_size("dp")
    far = n_dp // 2
    capacity = max(2, 5 * tok * top // (4 * exp_dev * owners))
    capacity = -(-capacity // 16) * 16
    row_here = lax.axis_index("expert")
    z = lax.axis_index("dp")
    partner_here = jnp.sum(jnp.where(jnp.arange(owners) == row_here, partner, 0))
    half = units // far
    part_at = (z // 2) * half

    spare = -(2 * top) % 8
    aux = jnp.concatenate([router_probs.T, routes.T.astype(F32), jnp.zeros((spare, tok), F32)])
    x_all, c_all, aux_all = gather(tokens, cotangent, aux, owners, n_dp)

    quarter = half // 2
    mine = lax.rem(z, 2)
    near = [(i, i ^ 1) for i in range(n_dp)]
    across = [(i, i ^ (owners // 2)) for i in range(owners)]
    picks, later, pieces, sums = [], [], [], []
    for s in range(exp_dev):
        expert = (partner_here * exp_dev + s).astype(F32)
        gate_w, up_w, down_w = gate_weight[s], up_weight[s], down_weight[s]
        lists = ([], [], [])
        rows = []
        for h in range(far):
            probs, names = aux_all[h, :, :top], aux_all[h, :, top : 2 * top]
            chosen, row_prob = select(names, probs, expert, capacity)
            if h == 0:
                picks.append(chosen)
            if pieces:
                chosen, _ = lax.optimization_barrier((chosen, tuple(pieces)))
            x = pick(chosen, x_all[h]).astype(BF)
            c = (pick(chosen, c_all[h]) * row_prob).astype(BF)
            if h == 0:
                dgate, dup, hidden = acts(x, c, gate_w, up_w, down_w)
                later.append((dgate, dup, hidden, row_prob))
                dgate, dup, hidden = (
                    lax.dynamic_slice_in_dim(v, part_at, half, 1) for v in (dgate, dup, hidden)
                )
            else:
                dgate, dup, hidden = acts(
                    x,
                    c,
                    lax.dynamic_slice_in_dim(gate_w, part_at, half, 1),
                    lax.dynamic_slice_in_dim(up_w, part_at, half, 1),
                    lax.dynamic_slice_in_dim(down_w, part_at, half, 0),
                )
            for kept, v in zip(lists, (dgate, dup, hidden)):
                kept.append(v)
            rows.append((x, x, c))
        for m in range(3):
            total = None
            for h in range(far):
                term = dot(lists[m][h], rows[h][m], ((0,), (0,)))
                total = term if total is None else total + term
            piece = total.astype(BF)
            pieces.append(piece)
            kept = lax.dynamic_slice_in_dim(piece, mine * quarter, quarter, 0)
            sent = lax.dynamic_slice_in_dim(piece, (1 - mine) * quarter, quarter, 0)
            came = lax.ppermute(sent, "dp", near)
            sums.append((kept.astype(F32) + came.astype(F32)).astype(BF))

    chosen = jnp.concatenate(picks, axis=1)
    outs, dxs = [], []
    for s in range(exp_dev):
        dgate, dup, hidden, row_prob = later[s]
        hidden, _ = lax.optimization_barrier((hidden, (*pieces, *sums[:3])))
        dgate, dup, _ = lax.optimization_barrier((dgate, dup, tuple(sums)))
        out = (dot(hidden, down_weight[s], ((1,), (0,))) * row_prob).astype(BF)
        dx = dot(dgate, gate_weight[s], ((1,), (1,))) + dot(dup, up_weight[s], ((1,), (1,)))
        outs.append(out.reshape(owners, capacity, width))
        dxs.append(dx.astype(BF).reshape(owners, capacity, width))

    def back(values):
        stacked = jnp.concatenate(values, axis=1)
        summed = lax.dot_general(
            chosen, stacked, (((1,), (1,)), ((0,), (0,))), preferred_element_type=F32
        ).astype(BF)
        return lax.psum_scatter(summed, "expert", scatter_dimension=0, tiled=False)

    output = back(outs)
    token_grad = back(dxs)

    finished = []
    for summed in sums:
        swapped = lax.ppermute(summed, "expert", across)
        finished.append(jnp.where(partner_here == row_here, summed, swapped))
    grads = jnp.stack(finished, axis=1).reshape(quarter, exp_dev, 3, width)
    return (output, token_grad, grads)


def solution(mesh):
    rows = P(("expert", "dp"), None)
    return jax.shard_map(
        local,
        mesh=mesh,
        in_specs=(rows, rows, rows, rows, P(), *[P("expert", None, None)] * 3),
        out_specs=(rows, rows, P("dp", "expert", None, None)),
        check_vma=False,
    )
```
